32 devices in a mesh: grp: 2 (over z_hi), seq: 8 (over y, x, core), tp: 2 (over z_lo).
Axes of the slice: x: 2, y: 2, z: 4 (z_hi: 2, z_lo: 2; z = z_hi * 2 + z_lo), core: 2. Of those that a mesh axis runs over, the one named last changes fastest.
Arguments:
- latents: bfloat16 [2, 64, 2048], P('grp', None, 'seq'), may hold values from -6 to 6
- patch_weight: bfloat16 [128, 5120], replicated, may hold values from -0.5 to 0.5
- patch_bias: float32 [5120], replicated, may hold values from -3 to 3
- modulation: float32 [3, 5120], replicated, may hold values from -3 to 3
- qkv_weight: bfloat16 [5120, 3, 1024], P(None, None, 'seq'), may hold values from -0.078125 to 0.078125
- norm_gain: float32 [2, 1024], P(None, 'seq'), may hold values from 0.5 to 16
- out_weight: bfloat16 [1024, 5120], P('seq', ('grp', 'tp')), may hold values from -0.5 to 0.5
- token_order: int32 [2048], replicated, may hold values from 0 to 2047, each once
- window_start: int32 [1], replicated, may hold values from 0 to 1024
Outputs:
- attended: bfloat16 [1024, 5120], P('seq', ('grp', 'tp'))
The draws below stay inside these ranges and needn't reach their ends.
Inputs may be any that keep to these rules, and one draw needn't show every extreme that they name: Position j of the target layout holds frame-major token token_order[j]; every token stands once. The window covers target positions window_start[0] to window_start[0] + 1023.
All inputs are finite; a program needn't handle non-finite values.
Results may differ from the reference program's by a relative error of at most 0.018.
The reference program's roundings to bfloat16 on the way (of `stacked`, `normed`, `values`, `probs_low` and `attention`) count: a program that leaves them out, or rounds other values in their place, can miss the bound.
Values may be sent and summed in bfloat16 or wider, within the bound.
A program may use at most 128 MiB of HBM per device.

```python
import math
import jax
import jax.numpy as jnp
from jax import lax

D = 5120
HD = 128
CH = 64
HEADS = 8
TOKENS = 2048
QWIN = 1024


def draw_norm_gain(key, part):
    total_width = HEADS * HD
    base = jnp.exp(jax.random.uniform(key, (2, total_width), jnp.float32, math.log(0.5), math.log(3.0)))
    return base


def level_of(key, extent, shards, least, high):
    gain = 1.0
    for dim, parts in shards:
        draws = jax.random.uniform(jax.random.fold_in(jax.random.fold_in(key, 6), dim), (parts,), jnp.float32, least / len(shards), high / len(shards))
        gain = gain * jnp.repeat(jnp.exp(draws), extent[dim] // parts).reshape((-1,) + (1,) * (len(extent) - 1 - dim))
    return gain


def bell_draw(rng, extent, scale, bound, split=(), kind=jnp.bfloat16):
    factor_of = level_of(rng, extent, split, -0.22, 0.18) if split else 1.0
    drawn = jax.random.normal(rng, extent, jnp.float32) * scale * factor_of
    return jnp.minimum(jnp.maximum(drawn, -bound), bound).astype(kind)


def setup_inputs(seed: int = 0) -> dict:
    splits = jax.random.split(jax.random.key(seed), 10)
    latents = bell_draw(splits[0], (2, CH, TOKENS), 1.0, 6.0, ((0, 2), (2, 8)))
    patch_weight = bell_draw(splits[1], (2 * CH, D), (2 * CH) ** -0.5, 0.5)
    patch_bias = bell_draw(splits[2], (D,), 0.5, 3.0, (), jnp.float32)
    modulation = bell_draw(splits[3], (3, D), 0.5, 3.0, (), jnp.float32)
    qkv_weight = bell_draw(splits[4], (D, 3, HEADS * HD), D ** -0.5, 0.078125, ((2, 8),))
    norm_gain = draw_norm_gain(jax.random.fold_in(splits[9], 71), 0)
    out_weight = bell_draw(splits[6], (HEADS * HD, D), HD ** -0.5, 0.5, ((0, 8), (1, 4)))
    token_order = jax.random.permutation(splits[7], TOKENS).astype(jnp.int32)
    window_start = jax.random.randint(splits[8], (1,), 0, TOKENS - QWIN + 1).astype(jnp.int32)
    return {"latents": latents, "patch_weight": patch_weight, "patch_bias": patch_bias, "modulation": modulation, "qkv_weight": qkv_weight, "norm_gain": norm_gain, "out_weight": out_weight, "token_order": token_order, "window_start": window_start}


norm_eps = 0.1

def reference(latents, patch_weight, patch_bias, modulation, qkv_weight, norm_gain, out_weight, token_order, window_start):
    stacked = jnp.concatenate([latents[0].T, latents[1].T], axis=1)
    embedded = jnp.dot(stacked, patch_weight, preferred_element_type=jnp.float32) + patch_bias
    centre = embedded - lax.optimization_barrier(jnp.mean(embedded, axis=1, keepdims=True))
    spread = lax.optimization_barrier(jnp.mean(centre * centre, axis=1, keepdims=True))
    normed = (centre * lax.rsqrt(spread + norm_eps) * (1.0 + modulation[1]) + modulation[0]).astype(jnp.bfloat16)
    window_rows = lax.dynamic_slice_in_dim(token_order, window_start[0], QWIN)
    picked = jnp.take(normed, window_rows, axis=0)
    query_raw = jnp.dot(picked, qkv_weight[:, 0, :], preferred_element_type=jnp.float32)
    key_raw = jnp.dot(normed, qkv_weight[:, 1, :], preferred_element_type=jnp.float32)
    values = jnp.dot(normed, qkv_weight[:, 2, :], preferred_element_type=jnp.float32).astype(jnp.bfloat16)
    query_mean = lax.optimization_barrier(jnp.mean(query_raw * query_raw, axis=1, keepdims=True))
    key_mean = lax.optimization_barrier(jnp.mean(key_raw * key_raw, axis=1, keepdims=True))
    queries = (query_raw * lax.rsqrt(query_mean + norm_eps) * norm_gain[0]).astype(jnp.bfloat16)
    keys = (key_raw * lax.rsqrt(key_mean + norm_eps) * norm_gain[1]).astype(jnp.bfloat16)
    head_queries = queries.reshape(QWIN, HEADS, HD).transpose(1, 0, 2)
    head_keys = keys.reshape(TOKENS, HEADS, HD).transpose(1, 0, 2)
    head_values = values.reshape(TOKENS, HEADS, HD).transpose(1, 0, 2)

    def attend(operands):
        query_head, key_head, value_head = operands
        scores = jnp.dot(query_head, key_head.T, preferred_element_type=jnp.float32) * HD ** (-0.5)
        probs = jnp.exp(scores - lax.optimization_barrier(jnp.max(scores, axis=1, keepdims=True)))
        probs_low = probs.astype(jnp.bfloat16)
        summed = jnp.dot(probs_low, value_head, preferred_element_type=jnp.float32)
        return (summed / lax.optimization_barrier(jnp.sum(probs, axis=1, keepdims=True))).astype(jnp.bfloat16)
    attention = lax.map(attend, (head_queries, head_keys, head_values))
    attention = attention.transpose(1, 0, 2).reshape(QWIN, HEADS * HD)
    mixed = jnp.dot(attention, out_weight, preferred_element_type=jnp.float32)
    return (mixed * modulation[2]).astype(jnp.bfloat16)
```

```python
import jax
import jax.numpy as jnp
from jax import lax
from jax.experimental import pallas as pl
from jax.experimental.pallas import tpu as pltpu
from jax.sharding import PartitionSpec as P

QW_DEV = 128
norm_eps = 0.1
MESH = pl.DeviceIdType.MESH
F32 = jnp.float32
BF16 = jnp.bfloat16


def flipped(index, mask):
    bit = 1
    while bit <= mask:
        if mask & bit:
            index = index + bit * (1 - 2 * ((index // bit) % 2))
        bit *= 2
    return index


def three_parts(x):
    high = x.astype(BF16).astype(F32)
    rest = x - high
    middle = rest.astype(BF16).astype(F32)
    return high, middle, rest - middle


def kernel(
    lat, pw, pb, mod, wq, gain, ow, rows, out,
    lat_all, x_aug, w_aug, centre, q_raw, k_raw, v_t, k_low,
    ss_all, q_all, part_acc, part_stat, got_acc, got_stat, att_z, att_x, ow_all,
    lat_s, lat_f, lat_r, ow_s, ow_l, ow_r, ss_s, ss_r, q_s, q_r,
    acc_s, acc_r, stat_s, stat_r, az_s, az_r, ax_s, ax_r,
):
    grp, seq, tp = lax.axis_index("grp"), lax.axis_index("seq"), lax.axis_index("tp")
    seq_n, tp_n = lax.axis_size("seq"), lax.axis_size("tp")
    groups = lax.axis_size("grp") * tp_n
    quarter = grp * tp_n + tp
    channels, local = lat.shape[1], lat.shape[2]
    width = pw.shape[1]
    hd = k_raw.shape[1]
    key_n = k_raw.shape[0]
    query_n = q_raw.shape[0]
    owners = seq_n // groups
    cols = ow.shape[1]

    def plane(index):
        return {"grp": grp, "seq": index, "tp": tp}

    def column(index):
        return {"grp": index // tp_n, "seq": seq, "tp": index % tp_n}

    def send(src, dst, send_sem, recv_sem, device):
        return pltpu.make_async_remote_copy(
            src_ref=src, dst_ref=dst, send_sem=send_sem, recv_sem=recv_sem,
            device_id=device, device_id_type=MESH,
        )

    def arrived(dst, sem):
        pltpu.make_async_copy(dst, dst, sem).wait()

    plane_peers = [flipped(seq, k) for k in range(1, seq_n)]
    column_peers = [(quarter + j) % groups for j in range(1, groups)]
    partner = {"grp": 1 - grp, "seq": seq, "tp": tp}
    core_mate = flipped(seq, 1)

    barrier = pltpu.get_barrier_semaphore()
    for peer in plane_peers:
        pl.semaphore_signal(barrier, inc=1, device_id=plane(peer), device_id_type=MESH)
    for peer in column_peers:
        pl.semaphore_signal(barrier, inc=1, device_id=column(peer), device_id_type=MESH)
    pl.semaphore_wait(barrier, len(plane_peers) + len(column_peers))

    pending = []

    def go(copy):
        copy.start()
        pending.append(copy)

    mine = lat_all.at[seq, grp]
    go(send(lat.at[0], mine, lat_s.at[0], lat_r.at[grp, seq], partner))
    for k, peer in enumerate(plane_peers):
        go(send(lat.at[0], mine, lat_s.at[k + 1], lat_r.at[grp, seq], plane(peer)))
    lat_all[seq, grp] = lat[0]

    w_aug[0 : 2 * channels, :] = pw[...]
    bias = pb[...]
    b_high, b_middle, b_low = three_parts(bias)
    line = lax.broadcasted_iota(jnp.int32, (16, width), 0)
    extra = jnp.where(line < 6, 1.0, 0.0)
    extra = jnp.where(line == 0, b_high, extra)
    extra = jnp.where(line == 1, b_middle, extra)
    extra = jnp.where(line == 2, b_low, extra)
    w_aug[2 * channels : 2 * channels + 16, :] = extra.astype(BF16)
    rest = w_aug.shape[0] - 2 * channels - 16
    w_aug[2 * channels + 16 :, :] = jnp.zeros((rest, width), BF16)
    w_mean = jnp.sum(pw[...].astype(F32), axis=1, keepdims=True) * (1.0 / width)
    b_mean = jnp.sum(bias, axis=1, keepdims=True) * (1.0 / width)

    other = lat_all.at[seq, 1 - grp]
    arrived(other, lat_r.at[1 - grp, seq])
    for k, peer in enumerate(plane_peers):
        go(send(other, other, lat_f.at[k], lat_r.at[1 - grp, seq], plane(peer)))

    ow_all[seq] = ow[...]
    go(send(ow, ow_all.at[seq], ow_s.at[0], ow_r.at[seq], plane(core_mate)))
    chips = seq_n // 2
    same_core = [flipped(seq, 2 * k) for k in range(1, chips)]
    early = [k for k in range(1, chips) if k & (k - 1) == 0]
    late = [k for k in range(1, chips) if k & (k - 1) != 0]
    for k in early:
        go(send(ow, ow_all.at[seq], ow_s.at[k], ow_r.at[seq], plane(same_core[k - 1])))

    wanted = rows[...]

    def picked(source, total):
        base = lax.broadcasted_iota(jnp.int32, (local, key_n), 0) + source * local
        hot = jnp.where(base == wanted, 1.0, 0.0).astype(BF16)
        block = lat_all[source].reshape(2 * channels, local)
        return total + jnp.dot(block, hot, preferred_element_type=F32)

    x_t = picked(seq, jnp.zeros((2 * channels, key_n), F32))
    for peer in plane_peers:
        arrived(lat_all.at[peer, grp], lat_r.at[grp, peer])
        arrived(lat_all.at[peer, 1 - grp], lat_r.at[1 - grp, peer])
        x_t = picked(peer, x_t)
    mean = jnp.sum(x_t * w_mean, axis=0, keepdims=True) + b_mean
    m_high, m_middle, m_low = three_parts(-mean)
    line = lax.broadcasted_iota(jnp.int32, (x_aug.shape[1] - 2 * channels, key_n), 0)
    extra = jnp.where(line < 3, 1.0, 0.0)
    extra = jnp.where(line == 3, m_high, extra)
    extra = jnp.where(line == 4, m_middle, extra)
    extra = jnp.where(line == 5, m_low, extra)
    x_aug[:, : 2 * channels] = x_t.T.astype(BF16)
    x_aug[:, 2 * channels :] = extra.T.astype(BF16)

    block = centre.shape[0]
    chunk = 1280 if width % 1280 == 0 else width
    mine_ss = ss_all.at[seq]
    key_lines = key_n // 128
    query_lines = query_n // 128
    for b in range(key_n // block):
        has_query = b * block < query_n
        first = 0 if has_query else 1
        x_block = x_aug[b * block : (b + 1) * block, :]

        def embed(c, total):
            at = pl.ds(pl.multiple_of(c * chunk, 128), chunk)
            e = jnp.dot(x_block, w_aug[:, at], preferred_element_type=F32)
            centre[:, at] = e
            sq = e * e
            for i in range(chunk // 128):
                total = total + sq[:, i * 128 : (i + 1) * 128]
            return total

        total = lax.fori_loop(0, width // chunk, embed, jnp.zeros((block, 128), F32))
        spread = jnp.sum(total, axis=1, keepdims=True) * (1.0 / width)
        factor = lax.rsqrt(spread + norm_eps)

        def project(c, total):
            at = pl.ds(pl.multiple_of(c * chunk, 128), chunk)
            normed = centre[:, at] * factor * (1.0 + mod[1:2, at]) + mod[0:1, at]
            weight = jnp.concatenate([wq[i, at, :] for i in range(first, 3)], axis=1)
            return total + jnp.dot(normed.astype(BF16), weight, preferred_element_type=F32)

        raw = lax.fori_loop(
            0, width // chunk, project, jnp.zeros((block, (3 - first) * hd), F32)
        )
        at = slice(b * block, (b + 1) * block)
        if has_query:
            q_raw[at, :] = raw[:, :hd]
        k_raw[at, :] = raw[:, (1 - first) * hd : (2 - first) * hd]
        v_t[:, at] = raw[:, (2 - first) * hd :].T.astype(BF16)

    for i in range(query_lines):
        piece = q_raw[i * 128 : (i + 1) * 128, :]
        mine_ss[i : i + 1, :] = jnp.sum((piece * piece).T, axis=0, keepdims=True)
    for i in range(key_lines):
        piece = k_raw[i * 128 : (i + 1) * 128, :]
        at = query_lines + i
        mine_ss[at : at + 1, :] = jnp.sum((piece * piece).T, axis=0, keepdims=True)
    if ss_all.shape[1] > query_lines + key_lines:
        left = ss_all.shape[1] - query_lines - key_lines
        mine_ss[query_lines + key_lines :, :] = jnp.zeros((left, 128), F32)
    for k, peer in enumerate(plane_peers):
        go(send(mine_ss, mine_ss, ss_s.at[k], ss_r.at[seq], plane(peer)))
    for k in late:
        go(send(ow, ow_all.at[seq], ow_s.at[k], ow_r.at[seq], plane(same_core[k - 1])))
    for peer in plane_peers:
        arrived(ss_all.at[peer], ss_r.at[peer])
    ss_total = ss_all[0]
    for i in range(1, seq_n):
        ss_total = ss_total + ss_all[i]
    inverse = lax.rsqrt(ss_total * (1.0 / (hd * seq_n)) + norm_eps).T
    for i in range(query_lines):
        at = slice(i * 128, (i + 1) * 128)
        piece = q_raw[at, :] * inverse[:, i : i + 1] * gain[0:1, :]
        q_all[quarter, :, at] = piece.T.astype(BF16)
    for j, peer in enumerate(column_peers):
        go(send(q_all.at[quarter], q_all.at[quarter], q_s.at[j], q_r.at[quarter], column(peer)))
    for i in range(key_lines):
        at = slice(i * 128, (i + 1) * 128)
        column_at = query_lines + i
        piece = k_raw[at, :] * inverse[:, column_at : column_at + 1] * gain[1:2, :]
        k_low[at, :] = piece.astype(BF16)

    scale = hd ** (-0.5)

    def attend(index):
        scores = jnp.dot(k_low[...], q_all[index], preferred_element_type=F32) * scale
        top = jnp.max(scores, axis=0, keepdims=True)
        probs = jnp.exp(scores - top)
        total = jnp.sum(probs, axis=0, keepdims=True)
        acc = jnp.dot(v_t[...], probs.astype(BF16), preferred_element_type=F32)
        return top, total, acc

    own = attend(quarter)
    for j, peer in enumerate(column_peers):
        arrived(q_all.at[peer], q_r.at[peer])
        top, total, acc = attend(peer)
        part_acc[j] = acc.astype(BF16)
        go(send(part_acc.at[j], got_acc.at[quarter], acc_s.at[j], acc_r.at[quarter], column(peer)))
        line = lax.broadcasted_iota(jnp.int32, (8, query_n), 0)
        part_stat[j] = jnp.where(line == 0, top, total)
        go(send(part_stat.at[j], got_stat.at[quarter], stat_s.at[j], stat_r.at[quarter], column(peer)))

    def relay(k):
        origin = same_core[k - 1]
        arrived(ow_all.at[origin], ow_r.at[origin])
        go(send(ow_all.at[origin], ow_all.at[origin], ow_l.at[k], ow_r.at[origin], plane(core_mate)))

    for k in early:
        relay(k)

    top, total, acc = own
    for peer in column_peers:
        arrived(got_stat.at[peer], stat_r.at[peer])
        arrived(got_acc.at[peer], acc_r.at[peer])
        peer_top = got_stat[peer, 0:1, :]
        peer_total = got_stat[peer, 1:2, :]
        both = jnp.maximum(top, peer_top)
        mine_factor = jnp.exp(top - both)
        peer_factor = jnp.exp(peer_top - both)
        total = total * mine_factor + peer_total * peer_factor
        acc = acc * mine_factor + got_acc[peer].astype(F32) * peer_factor
        top = both
    attention = (acc / total).T.astype(BF16)
    att_z[pl.ds(quarter * owners, owners)] = attention.reshape(owners, query_n // owners, hd)
    span = att_z.at[pl.ds(quarter * owners, owners)]
    for j, peer in enumerate(column_peers):
        go(send(span, span, az_s.at[j], az_r.at[quarter], column(peer)))

    def give(index):
        for i in range(owners):
            owner = index * owners + i

            @pl.when(owner != seq)
            def _():
                send(
                    att_z.at[owner], att_x.at[seq], ax_s.at[owner], ax_r.at[seq], plane(owner)
                ).start()

            @pl.when(owner == seq)
            def _():
                att_x[seq] = att_z[owner]

    give(quarter)
    for k in late:
        relay(k)
    for peer in column_peers:
        arrived(att_z.at[pl.ds(peer * owners, owners)], az_r.at[peer])
        give(peer)
    arrived(ow_all.at[core_mate], ow_r.at[core_mate])
    for k in range(1, chips):
        origin = flipped(core_mate, 2 * k)
        arrived(ow_all.at[origin], ow_r.at[origin])
    for peer in plane_peers:
        arrived(att_x.at[peer], ax_r.at[peer])
    lhs = jnp.concatenate([att_x[i] for i in range(seq_n)], axis=1)
    step = 256 if cols % 256 == 0 else cols
    for c in range(cols // step):
        at = slice(c * step, (c + 1) * step)
        mixed = jnp.dot(
            lhs, ow_all[:, :, at].reshape(seq_n * hd, step), preferred_element_type=F32
        )
        gate = mod[2:3, pl.ds(pl.multiple_of(quarter * cols + c * step, 128), step)]
        out[:, at] = (mixed * gate).astype(BF16)

    for copy in pending:
        copy.wait_send()
    for owner in range(seq_n):

        @pl.when(owner != seq)
        def _():
            send(
                att_z.at[owner], att_x.at[seq], ax_s.at[owner], ax_r.at[seq], plane(owner)
            ).wait_send()


def per_device(
    latents, patch_weight, patch_bias, modulation, qkv_weight, norm_gain, out_weight,
    token_order, window_start,
):
    seq_n = lax.axis_size("seq")
    tp_n = lax.axis_size("tp")
    groups = lax.axis_size("grp") * tp_n
    quarter = lax.axis_index("grp") * tp_n + lax.axis_index("tp")
    channels, local = latents.shape[1:]
    tokens = local * seq_n
    window = QW_DEV * seq_n
    width = patch_weight.shape[1]
    hd = qkv_weight.shape[2]
    cols = out_weight.shape[1]
    query_n = window // groups
    key_n = tokens // groups
    twice = jnp.concatenate([token_order, token_order])
    ordered = lax.dynamic_slice_in_dim(twice, window_start[0], tokens)
    rest_n = key_n - query_n
    rows = jnp.concatenate(
        [
            lax.dynamic_slice_in_dim(ordered, quarter * query_n, query_n),
            lax.dynamic_slice_in_dim(ordered, window + quarter * rest_n, rest_n),
        ]
    ).reshape(1, key_n)
    depth = 2 * channels + 128
    block = min(256, query_n)
    lines = -(-(key_n // 128 + query_n // 128) // 8) * 8
    dma = pltpu.SemaphoreType.DMA
    vmem = pl.BlockSpec(memory_space=pltpu.VMEM)
    return pl.pallas_call(
        kernel,
        out_shape=jax.ShapeDtypeStruct((QW_DEV, cols), BF16),
        in_specs=[vmem] * 8,
        out_specs=vmem,
        scratch_shapes=[
            pltpu.VMEM((seq_n, 2, channels, local), BF16),
            pltpu.VMEM((key_n, depth), BF16),
            pltpu.VMEM((depth, width), BF16),
            pltpu.VMEM((block, width), F32),
            pltpu.VMEM((query_n, hd), F32),
            pltpu.VMEM((key_n, hd), F32),
            pltpu.VMEM((hd, key_n), BF16),
            pltpu.VMEM((key_n, hd), BF16),
            pltpu.VMEM((seq_n, lines, 128), F32),
            pltpu.VMEM((groups, hd, query_n), BF16),
            pltpu.VMEM((groups - 1, hd, query_n), BF16),
            pltpu.VMEM((groups - 1, 8, query_n), F32),
            pltpu.VMEM((groups, hd, query_n), BF16),
            pltpu.VMEM((groups, 8, query_n), F32),
            pltpu.VMEM((seq_n, QW_DEV, hd), BF16),
            pltpu.VMEM((seq_n, QW_DEV, hd), BF16),
            pltpu.VMEM((seq_n, hd, cols), BF16),
            dma((seq_n,)), dma((seq_n,)), dma((2, seq_n)),
            dma((seq_n,)), dma((seq_n,)), dma((seq_n,)),
            dma((seq_n,)), dma((seq_n,)),
            dma((groups,)), dma((groups,)),
            dma((groups,)), dma((groups,)), dma((groups,)), dma((groups,)),
            dma((groups,)), dma((groups,)),
            dma((seq_n,)), dma((seq_n,)),
        ],
        compiler_params=pltpu.CompilerParams(
            collective_id=0, has_side_effects=True, vmem_limit_bytes=60 * 1024 * 1024
        ),
    )(
        latents,
        patch_weight,
        patch_bias.reshape(1, width),
        modulation,
        jnp.transpose(qkv_weight, (1, 0, 2)),
        norm_gain,
        out_weight,
        rows,
    )


def solution(mesh):
    in_specs = (
        P("grp", None, "seq"),
        P(),
        P(),
        P(),
        P(None, None, "seq"),
        P(None, "seq"),
        P("seq", ("grp", "tp")),
        P(),
        P(),
    )
    out_specs = P("seq", ("grp", "tp"))
    return jax.shard_map(
        per_device, mesh=mesh, in_specs=in_specs, out_specs=out_specs, check_vma=False
    )
```

```python
import jax
import jax.numpy as jnp
from jax import lax
from jax.experimental import pallas as pl
from jax.experimental.pallas import tpu as pltpu
from jax.sharding import PartitionSpec as P

QW_DEV = 128
norm_eps = 0.1
MESH = pl.DeviceIdType.MESH
F32 = jnp.float32
BF16 = jnp.bfloat16


def flipped(index, mask):
    bit = 1
    while bit <= mask:
        if mask & bit:
            index = index + bit * (1 - 2 * ((index // bit) % 2))
        bit *= 2
    return index


def three_parts(x):
    high = x.astype(BF16).astype(F32)
    rest = x - high
    middle = rest.astype(BF16).astype(F32)
    return high, middle, rest - middle


def kernel(
    lat, pw, pb, mod, wq_hbm, gain, ow, rows, out,
    lat_all, x_aug, w_aug, wq, centre, q_raw, k_raw, v_t, k_low,
    ssq_all, ssk_all, q_all, part_acc, part_stat, got_acc, got_stat, att_z, att_x, ow_all,
    load, lat_s, lat_f, lat_r, ow_s, ow_l, ow_r, ssq_s, ssq_r, ssk_s, ssk_r, q_s, q_r,
    acc_s, acc_r, stat_s, stat_r, az_s, az_r, ax_s, ax_r,
):
    grp, seq, tp = lax.axis_index("grp"), lax.axis_index("seq"), lax.axis_index("tp")
    seq_n, tp_n = lax.axis_size("seq"), lax.axis_size("tp")
    groups = lax.axis_size("grp") * tp_n
    quarter = grp * tp_n + tp
    channels, local = lat.shape[1], lat.shape[2]
    width = pw.shape[1]
    hd = k_raw.shape[1]
    key_n = k_raw.shape[0]
    query_n = q_raw.shape[0]
    owners = seq_n // groups
    cols = ow.shape[1]

    def plane(index):
        return {"grp": grp, "seq": index, "tp": tp}

    def column(index):
        return {"grp": index // tp_n, "seq": seq, "tp": index % tp_n}

    def send(src, dst, send_sem, recv_sem, device):
        return pltpu.make_async_remote_copy(
            src_ref=src, dst_ref=dst, send_sem=send_sem, recv_sem=recv_sem,
            device_id=device, device_id_type=MESH,
        )

    def arrived(dst, sem):
        pltpu.make_async_copy(dst, dst, sem).wait()

    plane_peers = [flipped(seq, k) for k in range(1, seq_n)]
    column_peers = [(quarter + j) % groups for j in range(1, groups)]
    partner = {"grp": 1 - grp, "seq": seq, "tp": tp}
    core_mate = flipped(seq, 1)

    pw_load = pltpu.make_async_copy(pw, w_aug.at[pl.ds(0, 2 * channels)], load.at[0])
    wq_load = pltpu.make_async_copy(wq_hbm, wq, load.at[1])
    ow_load = pltpu.make_async_copy(ow, ow_all.at[seq], load.at[2])
    pw_load.start()
    wq_load.start()
    ow_load.start()

    barrier = pltpu.get_barrier_semaphore()
    for peer in plane_peers:
        pl.semaphore_signal(barrier, inc=1, device_id=plane(peer), device_id_type=MESH)
    for peer in column_peers:
        pl.semaphore_signal(barrier, inc=1, device_id=column(peer), device_id_type=MESH)
    pl.semaphore_wait(barrier, len(plane_peers) + len(column_peers))

    pending = []

    def go(copy):
        copy.start()
        pending.append(copy)

    mine = lat_all.at[seq, grp]
    go(send(lat.at[0], mine, lat_s.at[0], lat_r.at[grp, seq], partner))
    for k, peer in enumerate(plane_peers):
        go(send(lat.at[0], mine, lat_s.at[k + 1], lat_r.at[grp, seq], plane(peer)))
    lat_all[seq, grp] = lat[0]

    bias = pb[...]
    b_high, b_middle, b_low = three_parts(bias)
    line = lax.broadcasted_iota(jnp.int32, (16, width), 0)
    extra = jnp.where(line < 6, 1.0, 0.0)
    extra = jnp.where(line == 0, b_high, extra)
    extra = jnp.where(line == 1, b_middle, extra)
    extra = jnp.where(line == 2, b_low, extra)
    w_aug[2 * channels : 2 * channels + 16, :] = extra.astype(BF16)
    rest = w_aug.shape[0] - 2 * channels - 16
    w_aug[2 * channels + 16 :, :] = jnp.zeros((rest, width), BF16)
    pw_load.wait()
    w_mean = jnp.sum(w_aug[0 : 2 * channels, :].astype(F32), axis=1, keepdims=True) * (1.0 / width)
    b_mean = jnp.sum(bias, axis=1, keepdims=True) * (1.0 / width)

    other = lat_all.at[seq, 1 - grp]
    arrived(other, lat_r.at[1 - grp, seq])
    for k, peer in enumerate(plane_peers):
        go(send(other, other, lat_f.at[k], lat_r.at[1 - grp, seq], plane(peer)))

    chips = seq_n // 2
    same_core = [flipped(seq, 2 * k) for k in range(1, chips)]
    early = [k for k in range(1, chips) if k & (k - 1) == 0]
    late = [k for k in range(1, chips) if k & (k - 1) != 0]
    half = hd // 2

    def give_weights(ks, h):
        part = pl.ds(h * half, half)
        for k in ks:
            peer = core_mate if k == 0 else same_core[k - 1]
            go(send(
                ow.at[part], ow_all.at[seq, part], ow_s.at[h, k], ow_r.at[h, seq], plane(peer)
            ))

    wanted = rows[...]

    def picked(source, total):
        base = lax.broadcasted_iota(jnp.int32, (local, key_n), 0) + source * local
        hot = jnp.where(base == wanted, 1.0, 0.0).astype(BF16)
        block = lat_all[source].reshape(2 * channels, local)
        return total + jnp.dot(block, hot, preferred_element_type=F32)

    x_t = picked(seq, jnp.zeros((2 * channels, key_n), F32))
    for peer in plane_peers:
        arrived(lat_all.at[peer, grp], lat_r.at[grp, peer])
        arrived(lat_all.at[peer, 1 - grp], lat_r.at[1 - grp, peer])
        x_t = picked(peer, x_t)
    give_weights([0] + early, 0)
    mean = jnp.sum(x_t * w_mean, axis=0, keepdims=True) + b_mean
    m_high, m_middle, m_low = three_parts(-mean)
    line = lax.broadcasted_iota(jnp.int32, (x_aug.shape[1] - 2 * channels, key_n), 0)
    extra = jnp.where(line < 3, 1.0, 0.0)
    extra = jnp.where(line == 3, m_high, extra)
    extra = jnp.where(line == 4, m_middle, extra)
    extra = jnp.where(line == 5, m_low, extra)
    x_aug[:, : 2 * channels] = x_t.T.astype(BF16)
    x_aug[:, 2 * channels :] = extra.T.astype(BF16)

    block = centre.shape[0]
    chunk = 1280 if width % 1280 == 0 else width
    key_lines = key_n // 128
    query_lines = query_n // 128

    def share(raw, lines, everyone, send_sem, recv_sem):
        for i in range(lines):
            piece = raw[i * 128 : (i + 1) * 128, :]
            everyone[seq, i : i + 1, :] = jnp.sum((piece * piece).T, axis=0, keepdims=True)
        if everyone.shape[1] > lines:
            everyone[seq, lines:, :] = jnp.zeros((everyone.shape[1] - lines, 128), F32)
        mine_ss = everyone.at[seq]
        for k, peer in enumerate(plane_peers):
            go(send(mine_ss, mine_ss, send_sem.at[k], recv_sem.at[seq], plane(peer)))

    def inverse_of(everyone, recv_sem):
        for peer in plane_peers:
            arrived(everyone.at[peer], recv_sem.at[peer])
        total = everyone[0]
        for i in range(1, seq_n):
            total = total + everyone[i]
        return lax.rsqrt(total * (1.0 / (hd * seq_n)) + norm_eps).T

    def send_queries():
        inverse = inverse_of(ssq_all, ssq_r)
        for i in range(query_lines):
            at = slice(i * 128, (i + 1) * 128)
            piece = q_raw[at, :] * inverse[:, i : i + 1] * gain[0:1, :]
            q_all[quarter, :, at] = piece.T.astype(BF16)
        mine_q = q_all.at[quarter]
        for j, peer in enumerate(column_peers):
            go(send(mine_q, mine_q, q_s.at[j], q_r.at[quarter], column(peer)))

    for b in range(key_n // block):
        has_query = b * block < query_n
        first = 0 if has_query else 1
        x_block = x_aug[b * block : (b + 1) * block, :]

        def embed(c, total):
            at = pl.ds(pl.multiple_of(c * chunk, 128), chunk)
            e = jnp.dot(x_block, w_aug[:, at], preferred_element_type=F32)
            centre[:, at] = e
            sq = e * e
            for i in range(chunk // 128):
                total = total + sq[:, i * 128 : (i + 1) * 128]
            return total

        total = lax.fori_loop(0, width // chunk, embed, jnp.zeros((block, 128), F32))
        spread = jnp.sum(total, axis=1, keepdims=True) * (1.0 / width)
        factor = lax.rsqrt(spread + norm_eps)
        if b == 0:
            wq_load.wait()
        if b * block == query_n:
            send_queries()

        def project(c, total):
            at = pl.ds(pl.multiple_of(c * chunk, 128), chunk)
            normed = centre[:, at] * factor * (1.0 + mod[1:2, at]) + mod[0:1, at]
            weight = jnp.concatenate([wq[i, at, :] for i in range(first, 3)], axis=1)
            return total + jnp.dot(normed.astype(BF16), weight, preferred_element_type=F32)

        raw = lax.fori_loop(
            0, width // chunk, project, jnp.zeros((block, (3 - first) * hd), F32)
        )
        at = slice(b * block, (b + 1) * block)
        if has_query:
            q_raw[at, :] = raw[:, :hd]
        k_raw[at, :] = raw[:, (1 - first) * hd : (2 - first) * hd]
        v_t[:, at] = raw[:, (2 - first) * hd :].T.astype(BF16)

        if (b + 1) * block == query_n:
            share(q_raw, query_lines, ssq_all, ssq_s, ssq_r)
            give_weights([0] + early, 1)
    if query_n == key_n:
        send_queries()
    share(k_raw, key_lines, ssk_all, ssk_s, ssk_r)
    for h in range(2):
        give_weights(late, h)
    inverse = inverse_of(ssk_all, ssk_r)
    for i in range(key_lines):
        at = slice(i * 128, (i + 1) * 128)
        piece = k_raw[at, :] * inverse[:, i : i + 1] * gain[1:2, :]
        k_low[at, :] = piece.astype(BF16)

    scale = hd ** (-0.5)

    def attend(index):
        scores = jnp.dot(k_low[...], q_all[index], preferred_element_type=F32) * scale
        top = jnp.max(scores, axis=0, keepdims=True)
        probs = jnp.exp(scores - top)
        total = jnp.sum(probs, axis=0, keepdims=True)
        acc = jnp.dot(v_t[...], probs.astype(BF16), preferred_element_type=F32)
        return top, total, acc

    own = attend(quarter)
    for j, peer in enumerate(column_peers):
        arrived(q_all.at[peer], q_r.at[peer])
        top, total, acc = attend(peer)
        part_acc[j] = acc.astype(BF16)
        go(send(part_acc.at[j], got_acc.at[quarter], acc_s.at[j], acc_r.at[quarter], column(peer)))
        line = lax.broadcasted_iota(jnp.int32, (8, query_n), 0)
        part_stat[j] = jnp.where(line == 0, top, total)
        go(send(part_stat.at[j], got_stat.at[quarter], stat_s.at[j], stat_r.at[quarter], column(peer)))

    def relay(k):
        origin = same_core[k - 1]
        for h in range(2):
            part = ow_all.at[origin, pl.ds(h * half, half)]
            arrived(part, ow_r.at[h, origin])
            go(send(part, part, ow_l.at[h, k], ow_r.at[h, origin], plane(core_mate)))

    for k in early:
        relay(k)

    top, total, acc = own
    for peer in column_peers:
        arrived(got_stat.at[peer], stat_r.at[peer])
        arrived(got_acc.at[peer], acc_r.at[peer])
        peer_top = got_stat[peer, 0:1, :]
        peer_total = got_stat[peer, 1:2, :]
        both = jnp.maximum(top, peer_top)
        mine_factor = jnp.exp(top - both)
        peer_factor = jnp.exp(peer_top - both)
        total = total * mine_factor + peer_total * peer_factor
        acc = acc * mine_factor + got_acc[peer].astype(F32) * peer_factor
        top = both
    attention = (acc / total).T.astype(BF16)
    att_z[pl.ds(quarter * owners, owners)] = attention.reshape(owners, query_n // owners, hd)
    span = att_z.at[pl.ds(quarter * owners, owners)]
    for j, peer in enumerate(column_peers):
        go(send(span, span, az_s.at[j], az_r.at[quarter], column(peer)))

    def give(index):
        for i in range(owners):
            owner = index * owners + i

            @pl.when(owner != seq)
            def _():
                send(
                    att_z.at[owner], att_x.at[seq], ax_s.at[owner], ax_r.at[seq], plane(owner)
                ).start()

            @pl.when(owner == seq)
            def _():
                att_x[seq] = att_z[owner]

    give(quarter)
    for k in late:
        relay(k)
    for peer in column_peers:
        arrived(att_z.at[pl.ds(peer * owners, owners)], az_r.at[peer])
        give(peer)
    ow_load.wait()
    for k in range(chips):
        origin = flipped(core_mate, 2 * k)
        for h in range(2):
            arrived(ow_all.at[origin, pl.ds(h * half, half)], ow_r.at[h, origin])
    for peer in plane_peers:
        arrived(att_x.at[peer], ax_r.at[peer])
    lhs = jnp.concatenate([att_x[i] for i in range(seq_n)], axis=1)
    step = 256 if cols % 256 == 0 else cols
    for c in range(cols // step):
        at = slice(c * step, (c + 1) * step)
        mixed = jnp.dot(
            lhs, ow_all[:, :, at].reshape(seq_n * hd, step), preferred_element_type=F32
        )
        gate = mod[2:3, pl.ds(pl.multiple_of(quarter * cols + c * step, 128), step)]
        out[:, at] = (mixed * gate).astype(BF16)

    for copy in pending:
        copy.wait_send()
    for owner in range(seq_n):

        @pl.when(owner != seq)
        def _():
            send(
                att_z.at[owner], att_x.at[seq], ax_s.at[owner], ax_r.at[seq], plane(owner)
            ).wait_send()


def per_device(
    latents, patch_weight, patch_bias, modulation, qkv_weight, norm_gain, out_weight,
    token_order, window_start,
):
    seq_n = lax.axis_size("seq")
    tp_n = lax.axis_size("tp")
    groups = lax.axis_size("grp") * tp_n
    quarter = lax.axis_index("grp") * tp_n + lax.axis_index("tp")
    channels, local = latents.shape[1:]
    tokens = local * seq_n
    window = QW_DEV * seq_n
    width = patch_weight.shape[1]
    hd = qkv_weight.shape[2]
    cols = out_weight.shape[1]
    query_n = window // groups
    key_n = tokens // groups
    rest_n = key_n - query_n
    start = window_start[0]
    before = lax.dynamic_slice_in_dim(token_order, quarter * rest_n, rest_n)
    behind = lax.dynamic_slice_in_dim(token_order, window + quarter * rest_n, rest_n)
    rest = jnp.where(quarter * rest_n + jnp.arange(rest_n) < start, before, behind)
    queries = lax.dynamic_slice_in_dim(token_order, start + quarter * query_n, query_n)
    rows = jnp.concatenate([queries, rest]).reshape(1, key_n)
    depth = 2 * channels + 128
    block = min(256, query_n)
    query_lines = -(-query_n // 1024) * 8
    key_lines = -(-key_n // 1024) * 8
    dma = pltpu.SemaphoreType.DMA
    vmem = pl.BlockSpec(memory_space=pltpu.VMEM)
    hbm = pl.BlockSpec(memory_space=pl.ANY)
    return pl.pallas_call(
        kernel,
        out_shape=jax.ShapeDtypeStruct((QW_DEV, cols), BF16),
        in_specs=[vmem, hbm, vmem, vmem, hbm, vmem, hbm, vmem],
        out_specs=vmem,
        scratch_shapes=[
            pltpu.VMEM((seq_n, 2, channels, local), BF16),
            pltpu.VMEM((key_n, depth), BF16),
            pltpu.VMEM((depth, width), BF16),
            pltpu.VMEM((3, width, hd), BF16),
            pltpu.VMEM((block, width), F32),
            pltpu.VMEM((query_n, hd), F32),
            pltpu.VMEM((key_n, hd), F32),
            pltpu.VMEM((hd, key_n), BF16),
            pltpu.VMEM((key_n, hd), BF16),
            pltpu.VMEM((seq_n, query_lines, 128), F32),
            pltpu.VMEM((seq_n, key_lines, 128), F32),
            pltpu.VMEM((groups, hd, query_n), BF16),
            pltpu.VMEM((groups - 1, hd, query_n), BF16),
            pltpu.VMEM((groups - 1, 8, query_n), F32),
            pltpu.VMEM((groups, hd, query_n), BF16),
            pltpu.VMEM((groups, 8, query_n), F32),
            pltpu.VMEM((seq_n, QW_DEV, hd), BF16),
            pltpu.VMEM((seq_n, QW_DEV, hd), BF16),
            pltpu.VMEM((seq_n, hd, cols), BF16),
            dma((3,)),
            dma((seq_n,)), dma((seq_n,)), dma((2, seq_n)),
            dma((2, seq_n)), dma((2, seq_n)), dma((2, seq_n)),
            dma((seq_n,)), dma((seq_n,)), dma((seq_n,)), dma((seq_n,)),
            dma((groups,)), dma((groups,)),
            dma((groups,)), dma((groups,)), dma((groups,)), dma((groups,)),
            dma((groups,)), dma((groups,)),
            dma((seq_n,)), dma((seq_n,)),
        ],
        compiler_params=pltpu.CompilerParams(
            collective_id=0, has_side_effects=True, vmem_limit_bytes=60 * 1024 * 1024
        ),
    )(
        latents,
        patch_weight,
        patch_bias.reshape(1, width),
        modulation,
        jnp.transpose(qkv_weight, (1, 0, 2)),
        norm_gain,
        out_weight,
        rows,
    )


def solution(mesh):
    in_specs = (
        P("grp", None, "seq"),
        P(),
        P(),
        P(),
        P(None, None, "seq"),
        P(None, "seq"),
        P("seq", ("grp", "tp")),
        P(),
        P(),
    )
    out_specs = P("seq", ("grp", "tp"))
    return jax.shard_map(
        per_device, mesh=mesh, in_specs=in_specs, out_specs=out_specs, check_vma=False
    )
```

```python
import jax
import jax.numpy as jnp
from jax import lax
from jax.experimental import pallas as pl
from jax.experimental.pallas import tpu as pltpu
from jax.sharding import PartitionSpec as P

QW_DEV = 128
norm_eps = 0.1
MESH = pl.DeviceIdType.MESH
F32 = jnp.float32
BF16 = jnp.bfloat16


def flipped(index, mask):
    bit = 1
    while bit <= mask:
        if mask & bit:
            index = index + bit * (1 - 2 * ((index // bit) % 2))
        bit *= 2
    return index


def three_parts(x):
    high = x.astype(BF16).astype(F32)
    rest = x - high
    middle = rest.astype(BF16).astype(F32)
    return high, middle, rest - middle


def kernel(
    lat, pw, pb, mod, wq_hbm, gain, ow, query_rows, rest_rows, out,
    lat_all, x_aug, w_aug, wq, centre, q_raw, k_raw, v_t, k_low,
    ssq_all, ssk_all, q_all, part_acc, part_stat, got_acc, got_stat, att_z, att_x, ow_all,
    load, lat_s, lat_f, lat_r, ow_s, ow_l, ow_r, ssq_s, ssq_r, ssk_s, ssk_r, q_s, q_r,
    acc_s, acc_r, stat_s, stat_r, az_s, az_r, ax_s, ax_r,
):
    grp, seq, tp = lax.axis_index("grp"), lax.axis_index("seq"), lax.axis_index("tp")
    seq_n, tp_n = lax.axis_size("seq"), lax.axis_size("tp")
    groups = lax.axis_size("grp") * tp_n
    quarter = grp * tp_n + tp
    channels, local = lat.shape[1], lat.shape[2]
    width = pw.shape[1]
    hd = k_raw.shape[1]
    key_n = k_raw.shape[0]
    query_n = q_raw.shape[0]
    owners = seq_n // groups
    cols = ow.shape[1]

    def plane(index):
        return {"grp": grp, "seq": index, "tp": tp}

    def column(index):
        return {"grp": index // tp_n, "seq": seq, "tp": index % tp_n}

    def send(src, dst, send_sem, recv_sem, device):
        return pltpu.make_async_remote_copy(
            src_ref=src, dst_ref=dst, send_sem=send_sem, recv_sem=recv_sem,
            device_id=device, device_id_type=MESH,
        )

    def arrived(dst, sem):
        pltpu.make_async_copy(dst, dst, sem).wait()

    plane_peers = [flipped(seq, k) for k in range(1, seq_n)]
    column_peers = [(quarter + j) % groups for j in range(1, groups)]
    partner = {"grp": 1 - grp, "seq": seq, "tp": tp}
    core_mate = flipped(seq, 1)

    pw_load = pltpu.make_async_copy(pw, w_aug.at[pl.ds(0, 2 * channels)], load.at[0])
    wq_load = pltpu.make_async_copy(wq_hbm, wq, load.at[1])
    ow_load = pltpu.make_async_copy(ow, ow_all.at[seq], load.at[2])
    pw_load.start()
    wq_load.start()
    ow_load.start()

    barrier = pltpu.get_barrier_semaphore()
    for peer in plane_peers:
        pl.semaphore_signal(barrier, inc=1, device_id=plane(peer), device_id_type=MESH)
    for peer in column_peers:
        pl.semaphore_signal(barrier, inc=1, device_id=column(peer), device_id_type=MESH)
    pl.semaphore_wait(barrier, len(plane_peers) + len(column_peers))

    pending = []

    def go(copy):
        copy.start()
        pending.append(copy)

    mine = lat_all.at[seq, grp]
    go(send(lat.at[0], mine, lat_s.at[0], lat_r.at[grp, seq], partner))
    for k, peer in enumerate(plane_peers):
        go(send(lat.at[0], mine, lat_s.at[k + 1], lat_r.at[grp, seq], plane(peer)))
    lat_all[seq, grp] = lat[0]

    bias = pb[...]
    b_high, b_middle, b_low = three_parts(bias)
    line = lax.broadcasted_iota(jnp.int32, (16, width), 0)
    extra = jnp.where(line < 6, 1.0, 0.0)
    extra = jnp.where(line == 0, b_high, extra)
    extra = jnp.where(line == 1, b_middle, extra)
    extra = jnp.where(line == 2, b_low, extra)
    w_aug[2 * channels : 2 * channels + 16, :] = extra.astype(BF16)
    rest = w_aug.shape[0] - 2 * channels - 16
    w_aug[2 * channels + 16 :, :] = jnp.zeros((rest, width), BF16)
    pw_load.wait()
    w_mean = jnp.sum(w_aug[0 : 2 * channels, :].astype(F32), axis=1, keepdims=True) * (1.0 / width)
    b_mean = jnp.sum(bias, axis=1, keepdims=True) * (1.0 / width)

    other = lat_all.at[seq, 1 - grp]
    arrived(other, lat_r.at[1 - grp, seq])
    for k, peer in enumerate(plane_peers):
        go(send(other, other, lat_f.at[k], lat_r.at[1 - grp, seq], plane(peer)))

    chips = seq_n // 2
    same_core = [flipped(seq, 2 * k) for k in range(1, chips)]
    early = [k for k in range(1, chips) if k & (k - 1) == 0]
    late = [k for k in range(1, chips) if k & (k - 1) != 0]
    half = hd // 2

    def give_weights(ks, h):
        part = pl.ds(h * half, half)
        for k in ks:
            peer = core_mate if k == 0 else same_core[k - 1]
            go(send(
                ow.at[part], ow_all.at[seq, part], ow_s.at[h, k], ow_r.at[h, seq], plane(peer)
            ))

    wanted = jnp.concatenate([query_rows[...], rest_rows[...]], axis=1)

    def picked(source, total):
        base = lax.broadcasted_iota(jnp.int32, (local, key_n), 0) + source * local
        hot = jnp.where(base == wanted, 1.0, 0.0).astype(BF16)
        block = lat_all[source].reshape(2 * channels, local)
        return total + jnp.dot(block, hot, preferred_element_type=F32)

    x_t = picked(seq, jnp.zeros((2 * channels, key_n), F32))
    for peer in plane_peers:
        arrived(lat_all.at[peer, grp], lat_r.at[grp, peer])
        arrived(lat_all.at[peer, 1 - grp], lat_r.at[1 - grp, peer])
        x_t = picked(peer, x_t)
    give_weights([0] + early, 0)
    mean = jnp.sum(x_t * w_mean, axis=0, keepdims=True) + b_mean
    m_high, m_middle, m_low = three_parts(-mean)
    line = lax.broadcasted_iota(jnp.int32, (x_aug.shape[1] - 2 * channels, key_n), 0)
    extra = jnp.where(line < 3, 1.0, 0.0)
    extra = jnp.where(line == 3, m_high, extra)
    extra = jnp.where(line == 4, m_middle, extra)
    extra = jnp.where(line == 5, m_low, extra)
    x_aug[:, : 2 * channels] = x_t.T.astype(BF16)
    x_aug[:, 2 * channels :] = extra.T.astype(BF16)

    block = centre.shape[0]
    chunk = 1280 if width % 1280 == 0 else width
    key_lines = key_n // 128
    query_lines = query_n // 128

    def share(raw, lines, everyone, send_sem, recv_sem):
        for i in range(lines):
            piece = raw[i * 128 : (i + 1) * 128, :]
            everyone[seq, i : i + 1, :] = jnp.sum((piece * piece).T, axis=0, keepdims=True)
        if everyone.shape[1] > lines:
            everyone[seq, lines:, :] = jnp.zeros((everyone.shape[1] - lines, 128), F32)
        mine_ss = everyone.at[seq]
        for k, peer in enumerate(plane_peers):
            go(send(mine_ss, mine_ss, send_sem.at[k], recv_sem.at[seq], plane(peer)))

    def inverse_of(everyone, recv_sem):
        for peer in plane_peers:
            arrived(everyone.at[peer], recv_sem.at[peer])
        total = everyone[0]
        for i in range(1, seq_n):
            total = total + everyone[i]
        return lax.rsqrt(total * (1.0 / (hd * seq_n)) + norm_eps).T

    def send_queries():
        inverse = inverse_of(ssq_all, ssq_r)
        for i in range(query_lines):
            at = slice(i * 128, (i + 1) * 128)
            piece = q_raw[at, :] * inverse[:, i : i + 1] * gain[0:1, :]
            q_all[quarter, :, at] = piece.T.astype(BF16)
        mine_q = q_all.at[quarter]
        for j, peer in enumerate(column_peers):
            go(send(mine_q, mine_q, q_s.at[j], q_r.at[quarter], column(peer)))

    for b in range(key_n // block):
        has_query = b * block < query_n
        first = 0 if has_query else 1
        x_block = x_aug[b * block : (b + 1) * block, :]

        def embed(c, total):
            at = pl.ds(pl.multiple_of(c * chunk, 128), chunk)
            e = jnp.dot(x_block, w_aug[:, at], preferred_element_type=F32)
            centre[:, at] = e
            sq = e * e
            for i in range(chunk // 128):
                total = total + sq[:, i * 128 : (i + 1) * 128]
            return total

        total = lax.fori_loop(0, width // chunk, embed, jnp.zeros((block, 128), F32))
        spread = jnp.sum(total, axis=1, keepdims=True) * (1.0 / width)
        factor = lax.rsqrt(spread + norm_eps)
        if b == 0:
            wq_load.wait()
        if b * block == query_n:
            send_queries()

        def project(c, total):
            at = pl.ds(pl.multiple_of(c * chunk, 128), chunk)
            normed = centre[:, at] * factor * (1.0 + mod[1:2, at]) + mod[0:1, at]
            weight = jnp.concatenate([wq[i, at, :] for i in range(first, 3)], axis=1)
            return total + jnp.dot(normed.astype(BF16), weight, preferred_element_type=F32)

        raw = lax.fori_loop(
            0, width // chunk, project, jnp.zeros((block, (3 - first) * hd), F32)
        )
        at = slice(b * block, (b + 1) * block)
        if has_query:
            q_raw[at, :] = raw[:, :hd]
        k_raw[at, :] = raw[:, (1 - first) * hd : (2 - first) * hd]
        v_t[:, at] = raw[:, (2 - first) * hd :].T.astype(BF16)

        if (b + 1) * block == query_n:
            share(q_raw, query_lines, ssq_all, ssq_s, ssq_r)
            give_weights([0] + early, 1)
    if query_n == key_n:
        send_queries()
    share(k_raw, key_lines, ssk_all, ssk_s, ssk_r)
    for h in range(2):
        give_weights(late, h)
    inverse = inverse_of(ssk_all, ssk_r)
    for i in range(key_lines):
        at = slice(i * 128, (i + 1) * 128)
        piece = k_raw[at, :] * inverse[:, i : i + 1] * gain[1:2, :]
        k_low[at, :] = piece.astype(BF16)

    scale = hd ** (-0.5)

    def attend(index):
        scores = jnp.dot(k_low[...], q_all[index], preferred_element_type=F32) * scale
        top = jnp.max(scores, axis=0, keepdims=True)
        probs = jnp.exp(scores - top)
        total = jnp.sum(probs, axis=0, keepdims=True)
        acc = jnp.dot(v_t[...], probs.astype(BF16), preferred_element_type=F32)
        return top, total, acc

    own = attend(quarter)
    for j, peer in enumerate(column_peers):
        arrived(q_all.at[peer], q_r.at[peer])
        top, total, acc = attend(peer)
        part_acc[j] = acc.astype(BF16)
        go(send(part_acc.at[j], got_acc.at[quarter], acc_s.at[j], acc_r.at[quarter], column(peer)))
        line = lax.broadcasted_iota(jnp.int32, (8, query_n), 0)
        part_stat[j] = jnp.where(line == 0, top, total)
        go(send(part_stat.at[j], got_stat.at[quarter], stat_s.at[j], stat_r.at[quarter], column(peer)))

    def relay(k):
        origin = same_core[k - 1]
        for h in range(2):
            part = ow_all.at[origin, pl.ds(h * half, half)]
            arrived(part, ow_r.at[h, origin])
            go(send(part, part, ow_l.at[h, k], ow_r.at[h, origin], plane(core_mate)))

    for k in early:
        relay(k)

    top, total, acc = own
    for peer in column_peers:
        arrived(got_stat.at[peer], stat_r.at[peer])
        arrived(got_acc.at[peer], acc_r.at[peer])
        peer_top = got_stat[peer, 0:1, :]
        peer_total = got_stat[peer, 1:2, :]
        both = jnp.maximum(top, peer_top)
        mine_factor = jnp.exp(top - both)
        peer_factor = jnp.exp(peer_top - both)
        total = total * mine_factor + peer_total * peer_factor
        acc = acc * mine_factor + got_acc[peer].astype(F32) * peer_factor
        top = both
    attention = (acc / total).T.astype(BF16)
    att_z[pl.ds(quarter * owners, owners)] = attention.reshape(owners, query_n // owners, hd)
    span = att_z.at[pl.ds(quarter * owners, owners)]
    for j, peer in enumerate(column_peers):
        go(send(span, span, az_s.at[j], az_r.at[quarter], column(peer)))

    def give(index):
        for i in range(owners):
            owner = index * owners + i

            @pl.when(owner != seq)
            def _():
                send(
                    att_z.at[owner], att_x.at[seq], ax_s.at[owner], ax_r.at[seq], plane(owner)
                ).start()

            @pl.when(owner == seq)
            def _():
                att_x[seq] = att_z[owner]

    give(quarter)
    for k in late:
        relay(k)
    for peer in column_peers:
        arrived(att_z.at[pl.ds(peer * owners, owners)], az_r.at[peer])
        give(peer)
    ow_load.wait()
    for k in range(chips):
        origin = flipped(core_mate, 2 * k)
        for h in range(2):
            arrived(ow_all.at[origin, pl.ds(h * half, half)], ow_r.at[h, origin])
    for peer in plane_peers:
        arrived(att_x.at[peer], ax_r.at[peer])
    lhs = jnp.concatenate([att_x[i] for i in range(seq_n)], axis=1)
    step = 256 if cols % 256 == 0 else cols
    for c in range(cols // step):
        at = slice(c * step, (c + 1) * step)
        mixed = jnp.dot(
            lhs, ow_all[:, :, at].reshape(seq_n * hd, step), preferred_element_type=F32
        )
        gate = mod[2:3, pl.ds(pl.multiple_of(quarter * cols + c * step, 128), step)]
        out[:, at] = (mixed * gate).astype(BF16)

    for copy in pending:
        copy.wait_send()
    for owner in range(seq_n):

        @pl.when(owner != seq)
        def _():
            send(
                att_z.at[owner], att_x.at[seq], ax_s.at[owner], ax_r.at[seq], plane(owner)
            ).wait_send()


def per_device(
    latents, patch_weight, patch_bias, modulation, qkv_weight, norm_gain, out_weight,
    token_order, window_start,
):
    seq_n = lax.axis_size("seq")
    tp_n = lax.axis_size("tp")
    groups = lax.axis_size("grp") * tp_n
    quarter = lax.axis_index("grp") * tp_n + lax.axis_index("tp")
    channels, local = latents.shape[1:]
    tokens = local * seq_n
    window = QW_DEV * seq_n
    width = patch_weight.shape[1]
    hd = qkv_weight.shape[2]
    cols = out_weight.shape[1]
    query_n = window // groups
    key_n = tokens // groups
    rest_n = key_n - query_n
    start = window_start[0]
    before = lax.dynamic_slice_in_dim(token_order, quarter * rest_n, rest_n)
    behind = lax.dynamic_slice_in_dim(token_order, window + quarter * rest_n, rest_n)
    rest = jnp.where(quarter * rest_n + jnp.arange(rest_n) < start, before, behind)
    queries = lax.dynamic_slice_in_dim(token_order, start + quarter * query_n, query_n)
    depth = 2 * channels + 128
    block = min(256, query_n)
    query_lines = -(-query_n // 1024) * 8
    key_lines = -(-key_n // 1024) * 8
    dma = pltpu.SemaphoreType.DMA
    vmem = pl.BlockSpec(memory_space=pltpu.VMEM)
    hbm = pl.BlockSpec(memory_space=pl.ANY)
    return pl.pallas_call(
        kernel,
        out_shape=jax.ShapeDtypeStruct((QW_DEV, cols), BF16),
        in_specs=[vmem, hbm, vmem, vmem, hbm, vmem, hbm, vmem, vmem],
        out_specs=vmem,
        scratch_shapes=[
            pltpu.VMEM((seq_n, 2, channels, local), BF16),
            pltpu.VMEM((key_n, depth), BF16),
            pltpu.VMEM((depth, width), BF16),
            pltpu.VMEM((3, width, hd), BF16),
            pltpu.VMEM((block, width), F32),
            pltpu.VMEM((query_n, hd), F32),
            pltpu.VMEM((key_n, hd), F32),
            pltpu.VMEM((hd, key_n), BF16),
            pltpu.VMEM((key_n, hd), BF16),
            pltpu.VMEM((seq_n, query_lines, 128), F32),
            pltpu.VMEM((seq_n, key_lines, 128), F32),
            pltpu.VMEM((groups, hd, query_n), BF16),
            pltpu.VMEM((groups - 1, hd, query_n), BF16),
            pltpu.VMEM((groups - 1, 8, query_n), F32),
            pltpu.VMEM((groups, hd, query_n), BF16),
            pltpu.VMEM((groups, 8, query_n), F32),
            pltpu.VMEM((seq_n, QW_DEV, hd), BF16),
            pltpu.VMEM((seq_n, QW_DEV, hd), BF16),
            pltpu.VMEM((seq_n, hd, cols), BF16),
            dma((3,)),
            dma((seq_n,)), dma((seq_n,)), dma((2, seq_n)),
            dma((2, seq_n)), dma((2, seq_n)), dma((2, seq_n)),
            dma((seq_n,)), dma((seq_n,)), dma((seq_n,)), dma((seq_n,)),
            dma((groups,)), dma((groups,)),
            dma((groups,)), dma((groups,)), dma((groups,)), dma((groups,)),
            dma((groups,)), dma((groups,)),
            dma((seq_n,)), dma((seq_n,)),
        ],
        compiler_params=pltpu.CompilerParams(
            collective_id=0, has_side_effects=True, vmem_limit_bytes=60 * 1024 * 1024
        ),
    )(
        latents,
        patch_weight,
        patch_bias.reshape(1, width),
        modulation,
        jnp.transpose(qkv_weight, (1, 0, 2)),
        norm_gain,
        out_weight,
        queries.reshape(1, query_n),
        rest.reshape(1, rest_n),
    )


def solution(mesh):
    in_specs = (
        P("grp", None, "seq"),
        P(),
        P(),
        P(),
        P(None, None, "seq"),
        P(None, "seq"),
        P("seq", ("grp", "tp")),
        P(),
        P(),
    )
    out_specs = P("seq", ("grp", "tp"))
    return jax.shard_map(
        per_device, mesh=mesh, in_specs=in_specs, out_specs=out_specs, check_vma=False
    )
```
